32 devices in a mesh: grp: 4 (over y, x), span: 8 (over z, core).
Axes of the slice: x: 2, y: 2, z: 4, core: 2. Of those that a mesh axis runs over, the one named last changes fastest.
Arguments:
- traces: bfloat16 [1024, 61440], P('grp', 'span'), may hold values from -1200 to 1200
- seg_starts: int32 [16], replicated, may hold values from 0 to 57344, as said below
- pair_offsets: int32 [1024, 32], P(('grp', 'span')), may hold values from 1 to 64, as said below
Outputs:
- correlations: bfloat16 [1024, 32, 512], P(('grp', 'span'))
The draws below stay inside these ranges and needn't reach their ends.
Inputs may be any that keep to these rules, and one draw needn't show every extreme that they name: `seg_starts`: segments may intersect; one starts at 0 and one at 57344. `pair_offsets`: each channel lists 32 different offsets; its partner is the channel plus the offset.
All inputs are finite; a program needn't handle non-finite values.
Results may differ from the reference program's by a relative error of at most 0.015.
Values may be sent and summed in bfloat16 or wider, within the bound.
A program may use at most 128 MiB of HBM per device.

```python
import math
import jax
import jax.numpy as jnp
from jax import lax

CH_GRP = 256
L = 4096
BINS = 1024
BIN0 = 64
HALF = 32
LAGS = 512
MAXOFF = 64
NPART = 32
SEGS = 16
SAMPLES = 61440
CHANNELS = 1024
N_GRP = 4


def draw_traces(key, part):
    key_noise = jax.random.fold_in(key, 11)
    key_gain = jax.random.fold_in(key, 12)
    key_colour = jax.random.fold_in(key, 13)
    key_envelope = jax.random.fold_in(key, 15)
    white_noise = jnp.clip(jax.random.normal(key_noise, (CHANNELS, SAMPLES + 1), jnp.float32), -4.0, 4.0)
    channel_gain = jnp.exp(jax.random.uniform(key_gain, (CHANNELS, 1), jnp.float32, 0.0, math.log(10.0)))
    colour = jax.random.uniform(key_colour, (CHANNELS, 1), jnp.float32, -0.9, 0.9)
    block_count = (SAMPLES + 127) // 128
    envelope = jnp.exp(jax.random.uniform(key_envelope, (1, block_count), jnp.float32, 0.0, math.log(10.0)))
    envelope = jnp.repeat(envelope, 128, axis=1)[:, :SAMPLES]
    values = channel_gain * envelope * (white_noise[:, 1:] + colour * white_noise[:, :-1])
    return values.astype(jnp.bfloat16)


def draw_seg_starts(key, part):
    starts_drawn = jax.random.randint(jax.random.fold_in(key, 3), (SEGS,), 0, SAMPLES - L + 1, dtype=jnp.int32)
    return starts_drawn.at[0].set(0).at[1].set(SAMPLES - L)


def draw_pair_offsets(key, part):
    scores = jax.random.randint(jax.random.fold_in(key, 5), (CHANNELS, MAXOFF), 0, 1 << 20, dtype=jnp.int32) * 128
    scores = scores + jnp.arange(MAXOFF, dtype=jnp.int32)[None, :]
    scores = scores.at[0, 0].set(-2).at[0, MAXOFF - 1].set(-1)
    ranking = jnp.argsort(scores, axis=1)[:, :NPART]
    return (ranking + 1).astype(jnp.int32)


def setup_inputs(seed: int = 0) -> dict:
    keys = jax.random.split(jax.random.key(seed), 4)
    traces = draw_traces(jax.random.fold_in(keys[3], 71), 0)
    seg_starts = draw_seg_starts(jax.random.fold_in(keys[3], 71), 0)
    pair_offsets = draw_pair_offsets(jax.random.fold_in(keys[3], 71), 0)
    return dict(traces=traces, seg_starts=seg_starts, pair_offsets=pair_offsets)


def taper_window():
    sample_index = jnp.arange(L, dtype=jnp.float32)
    return 0.5 - 0.5 * jnp.cos(2.0 * math.pi / L * (sample_index + 0.5))

def whiten(real_part, imag_part):
    power_sum = real_part * real_part + imag_part * imag_part
    smooth = lax.reduce_window(power_sum, jnp.array(0.0, power_sum.dtype), lax.add, (1, 1, 2 * HALF + 1), (1, 1, 1), 'VALID') / (2 * HALF + 1)
    inverse = lax.rsqrt(smooth + 1e-06)
    band_real = real_part[..., HALF:HALF + BINS] * inverse
    band_imag = imag_part[..., HALF:HALF + BINS] * inverse
    return jnp.stack([band_real, band_imag], axis=1).astype(jnp.bfloat16)

def group_spectra(channel_rows, seg_starts):
    segments = jax.vmap(lambda seg_start: lax.dynamic_slice_in_dim(channel_rows, seg_start, L, 1), out_axes=1)(seg_starts)
    tapered = segments.astype(jnp.float32) * taper_window()
    transform = jnp.fft.rfft(tapered, axis=-1)[..., BIN0 - HALF:BIN0 + BINS + HALF]
    return whiten(jnp.real(transform).astype(jnp.float32), jnp.imag(transform).astype(jnp.float32))

def cross_spectra(own_rows, extended, offsets):
    row_total = own_rows.shape[0]
    block_rows = 16 if row_total % 16 == 0 else row_total
    halo_rows = extended.shape[0] - row_total

    def one_block(block_index):
        first_row = block_index * block_rows
        own_block = lax.dynamic_slice_in_dim(own_rows, first_row, block_rows, 0).astype(jnp.float32)
        others = lax.dynamic_slice_in_dim(extended, first_row, block_rows + halo_rows, 0).astype(jnp.float32)
        wanted = lax.dynamic_slice_in_dim(offsets, first_row, block_rows, 0)
        partner_index = (wanted + jnp.arange(block_rows, dtype=jnp.int32)[:, None]).astype(jnp.int32)
        rotated = jnp.stack([own_block[:, 1], -own_block[:, 0]], axis=1)
        gram_real = jnp.einsum('icsf,jcsf->ijf', own_block, others)
        gram_imag = jnp.einsum('icsf,jcsf->ijf', rotated, others)
        cross_real = jnp.take_along_axis(gram_real, partner_index[:, :, None], axis=1)
        cross_imag = jnp.take_along_axis(gram_imag, partner_index[:, :, None], axis=1)
        return jnp.stack([cross_real, cross_imag], axis=2)
    result = lax.map(one_block, jnp.arange(row_total // block_rows, dtype=jnp.int32))
    return result.reshape((row_total,) + result.shape[2:])

def lag_table():
    bin_index = jnp.arange(BINS, dtype=jnp.int32) + BIN0
    lag_index = jnp.arange(LAGS, dtype=jnp.int32) - LAGS // 2
    phase = jnp.mod(bin_index[:, None] * lag_index[None, :], L)
    angles = phase.astype(jnp.float32) * (2.0 * math.pi / L)
    return jnp.concatenate([jnp.cos(angles), -jnp.sin(angles)], axis=0).astype(jnp.bfloat16)

def reference(traces, seg_starts, pair_offsets):
    grouped = traces.reshape(N_GRP, CH_GRP, SAMPLES)
    spectra = lax.map(lambda channel_rows: group_spectra(channel_rows, seg_starts), grouped)
    spectra = spectra.reshape((CHANNELS,) + spectra.shape[2:])
    extended = jnp.concatenate([spectra, jnp.zeros((MAXOFF,) + spectra.shape[1:], jnp.bfloat16)], axis=0)
    cross_spec = cross_spectra(spectra, extended, pair_offsets).astype(jnp.bfloat16)
    flat_rows = cross_spec.reshape(CHANNELS * NPART, 2 * BINS)
    lag_scale = 1.0 / math.sqrt(SEGS * BINS)
    correlated = jnp.dot(flat_rows, lag_table(), preferred_element_type=jnp.float32) * lag_scale
    return correlated.reshape(CHANNELS, NPART, LAGS).astype(jnp.bfloat16)
```

```python
import functools
import math

import jax
import jax.numpy as jnp
import ml_dtypes
import numpy as np
from jax import lax
from jax.experimental import pallas as pl
from jax.experimental.pallas import tpu as pltpu
from jax.sharding import PartitionSpec as P

L = 4096
BINS = 1024
BIN0 = 64
HALF = 32
LAGS = 512
MAXOFF = 64

LANES = 128
WIDE = 1152
DEPTH = 512
STEPS = L // DEPTH
FOLD = BINS // LANES


def passed_along(block, axis, distance):
    devices = range(lax.axis_size(axis))
    route = [(i - distance, i) for i in devices if i - distance in devices]
    return lax.ppermute(block, axis, route)


@functools.cache
def column_bins():
    band = np.arange(BIN0, BIN0 + BINS)
    below = np.arange(BIN0 - HALF, BIN0)
    above = np.arange(BIN0 + BINS, BIN0 + BINS + HALF)
    return np.concatenate([band, below, above])


@functools.cache
def forward_tables():
    bins = column_bins()
    n = np.arange(L)
    angles = (n[:, None] * bins[None, :] % L) * (2.0 * np.pi / L)
    taper = (0.5 - 0.5 * np.cos(2.0 * np.pi / L * (n + 0.5)))[:, None]
    table = np.zeros((L, 2 * WIDE), np.float32)
    table[:, : len(bins)] = np.cos(angles) * taper
    table[:, WIDE : WIDE + len(bins)] = -np.sin(angles) * taper
    high = table.astype(ml_dtypes.bfloat16)
    low = (table - high.astype(np.float32)).astype(ml_dtypes.bfloat16)
    both = np.stack([high.reshape(STEPS, DEPTH, -1), low.reshape(STEPS, DEPTH, -1)], axis=1)
    return both.reshape(STEPS, 2 * DEPTH, 2 * WIDE)


@functools.cache
def band_table():
    bins = column_bins()
    band = np.zeros((WIDE, BINS), np.float32)
    centre = np.arange(BINS) + BIN0
    band[: len(bins)] = np.abs(bins[:, None] - centre[None, :]) <= HALF
    return band.astype(ml_dtypes.bfloat16)


@functools.cache
def lag_table():
    bins = np.arange(BINS) + BIN0
    lags = np.arange(LAGS) - LAGS // 2
    angles = (bins[:, None] * lags[None, :] % L) * (2.0 * np.pi / L)
    table = np.stack([np.cos(angles), -np.sin(angles)]).reshape(2, FOLD, LANES, LAGS)
    table = table.transpose(1, 0, 2, 3).reshape(FOLD, 2 * LANES, LAGS)
    return table.astype(np.float32).astype(ml_dtypes.bfloat16)


def spectra_kernel(starts_ref, rows_ref, table_ref, band_ref, out_ref, seg_ref, acc_ref):
    step = pl.program_id(0)
    channels, samples = rows_ref.shape
    lane = lax.broadcasted_iota(jnp.int32, (channels, LANES), 1)

    def one_segment(s, carry):
        start = starts_ref[s]
        within = lax.rem(start, LANES)
        first = start - within + step * DEPTH
        turn = lax.rem(LANES - within, LANES)
        row = pl.ds(pl.multiple_of(s * channels, channels), channels)
        turned = []
        for t in range(DEPTH // LANES + 1):
            at = jnp.minimum(first + t * LANES, samples - LANES)
            piece = rows_ref[:, pl.ds(pl.multiple_of(at, LANES), LANES)].astype(jnp.float32)
            turned.append(pltpu.roll(piece, turn, 1))
        for t in range(DEPTH // LANES):
            piece = jnp.where(lane < LANES - within, turned[t], turned[t + 1]).astype(jnp.bfloat16)
            seg_ref[row, t * LANES : (t + 1) * LANES] = piece
            seg_ref[row, DEPTH + t * LANES : DEPTH + (t + 1) * LANES] = piece
        return carry

    lax.fori_loop(0, starts_ref.shape[0], one_segment, 0)

    @pl.when(step == 0)
    def _():
        acc_ref[...] = jnp.zeros_like(acc_ref)

    for c in range(0, 2 * WIDE, 256):
        acc_ref[:, c : c + 256] += jnp.dot(
            seg_ref[...], table_ref[0, :, c : c + 256], preferred_element_type=jnp.float32
        )

    @pl.when(step == STEPS - 1)
    def _():
        block = 128

        def whiten(b, carry):
            row = pl.ds(pl.multiple_of(b * block, block), block)
            real = acc_ref[row, :WIDE]
            imag = acc_ref[row, WIDE:]
            power = real * real + imag * imag
            high = power.astype(jnp.bfloat16)
            low = (power - high.astype(jnp.float32)).astype(jnp.bfloat16)
            total = jnp.dot(high, band_ref[...], preferred_element_type=jnp.float32)
            total += jnp.dot(low, band_ref[...], preferred_element_type=jnp.float32)
            inverse = lax.rsqrt(total * (1.0 / (2 * HALF + 1)) + 1e-06)
            out_ref[0, row, :] = (real[:, :BINS] * inverse).astype(jnp.bfloat16)
            out_ref[1, row, :] = (imag[:, :BINS] * inverse).astype(jnp.bfloat16)
            return carry

        lax.fori_loop(0, acc_ref.shape[0] // block, whiten, 0)


def whitened(regrouped, seg_starts):
    channels, samples = regrouped.shape
    rows = channels * seg_starts.shape[0]
    return pl.pallas_call(
        spectra_kernel,
        grid=(STEPS,),
        in_specs=[
            pl.BlockSpec(memory_space=pltpu.SMEM),
            pl.BlockSpec((channels, samples), lambda j: (0, 0)),
            pl.BlockSpec((1, 2 * DEPTH, 2 * WIDE), lambda j: (j, 0, 0)),
            pl.BlockSpec((WIDE, BINS), lambda j: (0, 0)),
        ],
        out_specs=pl.BlockSpec((2, rows, BINS), lambda j: (0, 0, 0)),
        out_shape=jax.ShapeDtypeStruct((2, rows, BINS), jnp.bfloat16),
        scratch_shapes=[
            pltpu.VMEM((rows, 2 * DEPTH), jnp.bfloat16),
            pltpu.VMEM((rows, 2 * WIDE), jnp.float32),
        ],
        compiler_params=pltpu.CompilerParams(vmem_limit_bytes=56 * 2**20),
    )(seg_starts, regrouped, jnp.asarray(forward_tables()), jnp.asarray(band_table()))


def pairs_kernel(segs, channels, partners, scale, *refs):
    pieces = len(refs) - 6
    offsets_ref = refs[0]
    piece_refs = refs[1 : 1 + pieces]
    lag_ref, out_ref, ext_ref, real_ref, imag_ref = refs[1 + pieces :]
    total = pieces * channels
    block = out_ref.shape[0] // partners
    step = pl.program_id(0)

    @pl.when(step == 0)
    def _():
        for p, piece_ref in enumerate(piece_refs):

            def fill(ps, carry, p=p, piece_ref=piece_ref):
                row = pl.ds(pl.multiple_of(ps * channels, channels), channels)
                values = piece_ref[row, :].astype(jnp.float32)
                base = (ps * total + p * channels) * FOLD
                for g in range(FOLD):
                    ext_ref[pl.ds(base + g, channels, stride=FOLD), :] = values[
                        :, g * LANES : (g + 1) * LANES
                    ]
                return carry

            lax.fori_loop(0, 2 * segs, fill, 0)

    def tile(part, s, channel):
        at = ((part * segs + s) * total + channel) * FOLD
        return ext_ref[pl.ds(pl.multiple_of(at, FOLD), FOLD), :]

    together = 4

    def some_pairs(n, carry):
        local = n // (partners // together)
        k0 = lax.rem(n, partners // together) * together
        own = step * block + local
        others = [own + offsets_ref[own, k0 + u] for u in range(together)]
        reals = [None] * together
        imags = [None] * together
        for s in range(segs):
            ar = tile(0, s, own)
            ai = tile(1, s, own)
            for u in range(together):
                br = tile(0, s, others[u])
                bi = tile(1, s, others[u])
                real = ar * br + ai * bi
                imag = ai * br - ar * bi
                reals[u] = real if s == 0 else reals[u] + real
                imags[u] = imag if s == 0 else imags[u] + imag
        for u in range(together):
            at = pl.ds(pl.multiple_of((n * together + u) * FOLD, FOLD), FOLD)
            real_ref[at, :] = reals[u]
            imag_ref[at, :] = imags[u]
        return carry

    lax.fori_loop(0, block * partners // together, some_pairs, 0)

    rows = block * partners
    result = jnp.zeros((rows, LAGS), jnp.float32)
    for g in range(FOLD):
        real = real_ref[pl.ds(g, rows, stride=FOLD), :]
        imag = imag_ref[pl.ds(g, rows, stride=FOLD), :]
        both = jnp.concatenate([real, imag], axis=1).astype(jnp.bfloat16)
        result += jnp.dot(both, lag_ref[g], preferred_element_type=jnp.float32)
    out_ref[...] = (result * scale).astype(jnp.bfloat16)


def correlate(pieces, offsets, segs):
    channels, partners = offsets.shape
    block = 8 if channels % 8 == 0 else channels
    rows = block * partners
    total = len(pieces) * channels
    scale = 1.0 / math.sqrt(segs * BINS)
    return pl.pallas_call(
        functools.partial(pairs_kernel, segs, channels, partners, scale),
        grid=(channels // block,),
        in_specs=[pl.BlockSpec(memory_space=pltpu.SMEM)]
        + [pl.BlockSpec(piece.shape, lambda i: (0, 0)) for piece in pieces]
        + [pl.BlockSpec((FOLD, 2 * LANES, LAGS), lambda i: (0, 0, 0))],
        out_specs=pl.BlockSpec((rows, LAGS), lambda i: (i, 0)),
        out_shape=jax.ShapeDtypeStruct((channels * partners, LAGS), jnp.bfloat16),
        scratch_shapes=[
            pltpu.VMEM((2 * segs * total * FOLD, LANES), jnp.float32),
            pltpu.VMEM((rows * FOLD, LANES), jnp.float32),
            pltpu.VMEM((rows * FOLD, LANES), jnp.float32),
        ],
        compiler_params=pltpu.CompilerParams(vmem_limit_bytes=56 * 2**20),
    )(offsets, *pieces, jnp.asarray(lag_table()))


def on_device(traces, seg_starts, pair_offsets):
    regrouped = lax.all_to_all(traces, "span", split_axis=0, concat_axis=1, tiled=True)
    channels_here = regrouped.shape[0]
    segs = seg_starts.shape[0]
    spectra = whitened(regrouped, seg_starts).reshape(2 * segs * channels_here, BINS)
    pieces = [spectra]
    for distance in range(1, -(-MAXOFF // channels_here) + 1):
        pieces.append(passed_along(spectra, ("grp", "span"), -distance))
    result = correlate(pieces, pair_offsets, segs)
    return result.reshape(channels_here, pair_offsets.shape[1], LAGS)


def solution(mesh):
    placed = (P("grp", "span"), P(), P(("grp", "span"), None))
    return jax.shard_map(
        on_device,
        mesh=mesh,
        in_specs=placed,
        out_specs=P(("grp", "span"), None, None),
        check_vma=False,
    )
```

```python
import functools
import math

import jax
import jax.numpy as jnp
import ml_dtypes
import numpy as np
from jax import lax
from jax.experimental import pallas as pl
from jax.experimental.pallas import tpu as pltpu
from jax.sharding import PartitionSpec as P

L = 4096
BINS = 1024
BIN0 = 64
HALF = 32
LAGS = 512
MAXOFF = 64

LANES = 128
WIDE = 1152
DEPTH = 512
STEPS = L // DEPTH
FOLD = BINS // LANES
CHUNKS = 2


def passed_along(block, axis, distance):
    devices = range(lax.axis_size(axis))
    route = [(i - distance, i) for i in devices if i - distance in devices]
    return lax.ppermute(block, axis, route)


@functools.cache
def column_bins():
    band = np.arange(BIN0, BIN0 + BINS)
    below = np.arange(BIN0 - HALF, BIN0)
    above = np.arange(BIN0 + BINS, BIN0 + BINS + HALF)
    return np.concatenate([band, below, above])


@functools.cache
def forward_tables():
    bins = column_bins()
    n = np.arange(L)
    angles = (n[:, None] * bins[None, :] % L) * (2.0 * np.pi / L)
    taper = (0.5 - 0.5 * np.cos(2.0 * np.pi / L * (n + 0.5)))[:, None]
    table = np.zeros((L, 2 * WIDE), np.float32)
    table[:, : len(bins)] = np.cos(angles) * taper
    table[:, WIDE : WIDE + len(bins)] = -np.sin(angles) * taper
    high = table.astype(ml_dtypes.bfloat16)
    low = (table - high.astype(np.float32)).astype(ml_dtypes.bfloat16)
    both = np.stack([high.reshape(STEPS, DEPTH, -1), low.reshape(STEPS, DEPTH, -1)], axis=1)
    return both.reshape(STEPS, 2 * DEPTH, 2 * WIDE)


@functools.cache
def band_table():
    bins = column_bins()
    band = np.zeros((WIDE, BINS), np.float32)
    centre = np.arange(BINS) + BIN0
    band[: len(bins)] = np.abs(bins[:, None] - centre[None, :]) <= HALF
    return band.astype(ml_dtypes.bfloat16)


@functools.cache
def lag_table():
    bins = np.arange(BINS) + BIN0
    lags = np.arange(LAGS) - LAGS // 2
    angles = (bins[:, None] * lags[None, :] % L) * (2.0 * np.pi / L)
    table = np.stack([np.cos(angles), -np.sin(angles)]).reshape(2, FOLD, LANES, LAGS)
    table = table.transpose(1, 0, 2, 3).reshape(FOLD, 2 * LANES, LAGS)
    return table.astype(np.float32).astype(ml_dtypes.bfloat16)


def spectra_kernel(starts_ref, rows_ref, table_ref, band_ref, out_ref, seg_ref, acc_ref, tile_ref):
    step = pl.program_id(0)
    spans, channels, samples = rows_ref.shape
    columns = samples // LANES
    lane = lax.broadcasted_iota(jnp.int32, (channels, LANES), 1)

    def one_segment(s, carry):
        start = starts_ref[s]
        within = lax.rem(start, LANES)
        first = start // LANES + step * (DEPTH // LANES)
        turn = lax.rem(LANES - within, LANES)
        row = pl.ds(pl.multiple_of(s * channels, channels), channels)
        turned = []
        for t in range(DEPTH // LANES + 1):
            column = jnp.minimum(first + t, spans * columns - 1)
            at = pl.ds(pl.multiple_of(lax.rem(column, columns) * LANES, LANES), LANES)
            piece = rows_ref[column // columns, :, at].astype(jnp.float32)
            turned.append(pltpu.roll(piece, turn, 1))
        for t in range(DEPTH // LANES):
            piece = jnp.where(lane < LANES - within, turned[t], turned[t + 1]).astype(jnp.bfloat16)
            seg_ref[row, t * LANES : (t + 1) * LANES] = piece
            seg_ref[row, DEPTH + t * LANES : DEPTH + (t + 1) * LANES] = piece
        return carry

    lax.fori_loop(0, starts_ref.shape[0], one_segment, 0)

    @pl.when(step == 0)
    def _():
        acc_ref[...] = jnp.zeros_like(acc_ref)

    for c in range(0, 2 * WIDE, 256):
        acc_ref[:, c : c + 256] += jnp.dot(
            seg_ref[...], table_ref[0, :, c : c + 256], preferred_element_type=jnp.float32
        )

    @pl.when(step == STEPS - 1)
    def _():
        block = tile_ref.shape[1] // FOLD

        def whiten(b, carry):
            row = pl.ds(pl.multiple_of(b * block, block), block)
            real = acc_ref[row, :WIDE]
            imag = acc_ref[row, WIDE:]
            power = real * real + imag * imag
            high = power.astype(jnp.bfloat16)
            low = (power - high.astype(jnp.float32)).astype(jnp.bfloat16)
            total = jnp.dot(high, band_ref[...], preferred_element_type=jnp.float32)
            total += jnp.dot(low, band_ref[...], preferred_element_type=jnp.float32)
            inverse = lax.rsqrt(total * (1.0 / (2 * HALF + 1)) + 1e-06)
            tiles = pl.ds(pl.multiple_of(b * block * FOLD, block * FOLD), block * FOLD)
            for part, values in enumerate((real, imag)):
                scaled = values[:, :BINS] * inverse
                for g in range(FOLD):
                    tile_ref[part, pl.ds(g, block, stride=FOLD), :] = scaled[
                        :, g * LANES : (g + 1) * LANES
                    ]
                out_ref[part, tiles, :] = tile_ref[part].astype(jnp.bfloat16)
            return carry

        lax.fori_loop(0, acc_ref.shape[0] // block, whiten, 0)


def whitened(regrouped, seg_starts):
    _, channels, _ = regrouped.shape
    rows = channels * seg_starts.shape[0]
    return pl.pallas_call(
        spectra_kernel,
        grid=(STEPS,),
        in_specs=[
            pl.BlockSpec(memory_space=pltpu.SMEM),
            pl.BlockSpec(regrouped.shape, lambda j: (0, 0, 0)),
            pl.BlockSpec((1, 2 * DEPTH, 2 * WIDE), lambda j: (j, 0, 0)),
            pl.BlockSpec((WIDE, BINS), lambda j: (0, 0)),
        ],
        out_specs=pl.BlockSpec((2, rows * FOLD, LANES), lambda j: (0, 0, 0)),
        out_shape=jax.ShapeDtypeStruct((2, rows * FOLD, LANES), jnp.bfloat16),
        scratch_shapes=[
            pltpu.VMEM((rows, 2 * DEPTH), jnp.bfloat16),
            pltpu.VMEM((rows, 2 * WIDE), jnp.float32),
            pltpu.VMEM((2, 128 * FOLD, LANES), jnp.float32),
        ],
        compiler_params=pltpu.CompilerParams(vmem_limit_bytes=56 * 2**20),
        cost_estimate=pl.CostEstimate(
            flops=2 * rows * 2 * L * 2 * WIDE, transcendentals=0, bytes_accessed=80 * 2**20
        ),
    )(seg_starts, regrouped, jnp.asarray(forward_tables()), jnp.asarray(band_table()))


def pairs_kernel(segs, channels, partners, scale, *refs):
    pieces = len(refs) - 6
    offsets_ref = refs[0]
    piece_refs = refs[1 : 1 + pieces]
    lag_ref, out_ref, ext_ref, real_ref, imag_ref = refs[1 + pieces :]
    total = pieces * channels
    block = out_ref.shape[0] // partners
    step = pl.program_id(0)

    @pl.when(step == 0)
    def _():
        for p, piece_ref in enumerate(piece_refs):

            def fill(ps, carry, p=p, piece_ref=piece_ref):
                length = channels * FOLD
                source = pl.ds(pl.multiple_of(ps * length, length), length)
                base = pl.multiple_of((ps * total + p * channels) * FOLD, length)
                ext_ref[pl.ds(base, length), :] = piece_ref[source, :].astype(jnp.float32)
                return carry

            lax.fori_loop(0, 2 * segs, fill, 0)

    def tile(part, s, channel):
        at = ((part * segs + s) * total + channel) * FOLD
        return ext_ref[pl.ds(pl.multiple_of(at, FOLD), FOLD), :]

    together = 4

    def some_pairs(n, carry):
        local = n // (partners // together)
        k0 = lax.rem(n, partners // together) * together
        own = step * block + local
        others = [own + offsets_ref[own, k0 + u] for u in range(together)]
        reals = [None] * together
        imags = [None] * together
        for s in range(segs):
            ar = tile(0, s, own)
            ai = tile(1, s, own)
            for u in range(together):
                br = tile(0, s, others[u])
                bi = tile(1, s, others[u])
                real = ar * br + ai * bi
                imag = ai * br - ar * bi
                reals[u] = real if s == 0 else reals[u] + real
                imags[u] = imag if s == 0 else imags[u] + imag
        for u in range(together):
            at = pl.ds(pl.multiple_of((n * together + u) * FOLD, FOLD), FOLD)
            real_ref[at, :] = reals[u]
            imag_ref[at, :] = imags[u]
        return carry

    lax.fori_loop(0, block * partners // together, some_pairs, 0)

    rows = block * partners
    result = jnp.zeros((rows, LAGS), jnp.float32)
    for g in range(FOLD):
        real = real_ref[pl.ds(g, rows, stride=FOLD), :]
        imag = imag_ref[pl.ds(g, rows, stride=FOLD), :]
        both = jnp.concatenate([real, imag], axis=1).astype(jnp.bfloat16)
        result += jnp.dot(both, lag_ref[g], preferred_element_type=jnp.float32)
    out_ref[...] = (result * scale).astype(jnp.bfloat16)


def correlate(pieces, offsets, segs):
    channels, partners = offsets.shape
    block = 8 if channels % 8 == 0 else channels
    rows = block * partners
    total = len(pieces) * channels
    scale = 1.0 / math.sqrt(segs * BINS)
    return pl.pallas_call(
        functools.partial(pairs_kernel, segs, channels, partners, scale),
        grid=(channels // block,),
        in_specs=[pl.BlockSpec(memory_space=pltpu.SMEM)]
        + [pl.BlockSpec(piece.shape, lambda i: (0, 0)) for piece in pieces]
        + [pl.BlockSpec((FOLD, 2 * LANES, LAGS), lambda i: (0, 0, 0))],
        out_specs=pl.BlockSpec((rows, LAGS), lambda i: (i, 0)),
        out_shape=jax.ShapeDtypeStruct((channels * partners, LAGS), jnp.bfloat16),
        scratch_shapes=[
            pltpu.VMEM((2 * segs * total * FOLD, LANES), jnp.float32),
            pltpu.VMEM((rows * FOLD, LANES), jnp.float32),
            pltpu.VMEM((rows * FOLD, LANES), jnp.float32),
        ],
        compiler_params=pltpu.CompilerParams(vmem_limit_bytes=56 * 2**20),
        cost_estimate=pl.CostEstimate(
            flops=channels * partners * segs * 8 * BINS,
            transcendentals=0,
            bytes_accessed=80 * 2**20,
        ),
    )(offsets, *pieces, jnp.asarray(lag_table()))


def on_device(traces, seg_starts, pair_offsets):
    span = lax.axis_size("span")
    channels_here = traces.shape[0] // span
    segs = seg_starts.shape[0]
    chunk = channels_here // CHUNKS
    halo = MAXOFF // chunk
    by_chunk = traces.reshape(span, CHUNKS, chunk, traces.shape[1])
    pieces = []
    regrouped = []
    for h in range(CHUNKS):
        regrouped.append(
            lax.all_to_all(by_chunk[:, h], "span", split_axis=0, concat_axis=0, tiled=True)
        )
    for h in range(CHUNKS):
        rows = regrouped[h]
        if pieces:
            rows, pieces[-1] = lax.optimization_barrier((rows, pieces[-1]))
        spectra = whitened(rows, seg_starts)
        pieces.append(spectra.reshape(2 * segs * chunk * FOLD, LANES))
    last = CHUNKS + halo
    pieces += [None] * halo
    arrived = []
    for h in range(CHUNKS):
        piece = pieces[h]
        if arrived:
            piece = lax.optimization_barrier((piece, *arrived))[0]
        arrived = []
        for ahead in range(CHUNKS + h, last, CHUNKS):
            pieces[ahead] = passed_along(piece, ("grp", "span"), -(ahead // CHUNKS))
            arrived.append(pieces[ahead])
    results = []
    for h in range(CHUNKS):
        offsets = pair_offsets[h * chunk : (h + 1) * chunk]
        results.append(correlate(pieces[h : h + halo + 1], offsets, segs))
    result = jnp.concatenate(results, axis=0)
    return result.reshape(channels_here, pair_offsets.shape[1], LAGS)


def solution(mesh):
    placed = (P("grp", "span"), P(), P(("grp", "span"), None))
    return jax.shard_map(
        on_device,
        mesh=mesh,
        in_specs=placed,
        out_specs=P(("grp", "span"), None, None),
        check_vma=False,
    )
```

```python
import functools
import math

import jax
import jax.numpy as jnp
import ml_dtypes
import numpy as np
from jax import lax
from jax.experimental import pallas as pl
from jax.experimental.pallas import tpu as pltpu
from jax.sharding import PartitionSpec as P

L = 4096
BINS = 1024
BIN0 = 64
HALF = 32
LAGS = 512
MAXOFF = 64

LANES = 128
WIDE = 1152
DEPTH = 512
STEPS = L // DEPTH
FOLD = BINS // LANES
PAIR = 2 * FOLD
CHUNKS = 2


def passed_along(block, axis, distance):
    devices = range(lax.axis_size(axis))
    route = [(i - distance, i) for i in devices if i - distance in devices]
    return lax.ppermute(block, axis, route)


@functools.cache
def column_bins():
    band = np.arange(BIN0, BIN0 + BINS)
    below = np.arange(BIN0 - HALF, BIN0)
    above = np.arange(BIN0 + BINS, BIN0 + BINS + HALF)
    return np.concatenate([band, below, above])


@functools.cache
def forward_tables():
    bins = column_bins()
    n = np.arange(L)
    angles = (n[:, None] * bins[None, :] % L) * (2.0 * np.pi / L)
    taper = (0.5 - 0.5 * np.cos(2.0 * np.pi / L * (n + 0.5)))[:, None]
    table = np.zeros((L, 2 * WIDE), np.float32)
    table[:, : len(bins)] = np.cos(angles) * taper
    table[:, WIDE : WIDE + len(bins)] = -np.sin(angles) * taper
    high = table.astype(ml_dtypes.bfloat16)
    low = (table - high.astype(np.float32)).astype(ml_dtypes.bfloat16)
    both = np.stack([high.reshape(STEPS, DEPTH, -1), low.reshape(STEPS, DEPTH, -1)], axis=1)
    return both.reshape(STEPS, 2 * DEPTH, 2 * WIDE)


@functools.cache
def band_table():
    bins = column_bins()
    band = np.zeros((WIDE, BINS), np.float32)
    centre = np.arange(BINS) + BIN0
    band[: len(bins)] = np.abs(bins[:, None] - centre[None, :]) <= HALF
    return band.astype(ml_dtypes.bfloat16)


@functools.cache
def lag_table():
    bins = np.arange(BINS) + BIN0
    lags = np.arange(LAGS) - LAGS // 2
    angles = (bins[:, None] * lags[None, :] % L) * (2.0 * np.pi / L)
    table = np.stack([np.cos(angles), -np.sin(angles)]).reshape(2, FOLD, LANES, LAGS)
    table = table.transpose(1, 0, 2, 3).reshape(FOLD, 2 * LANES, LAGS)
    return table.astype(np.float32).astype(ml_dtypes.bfloat16)


def spectra_kernel(starts_ref, rows_ref, table_ref, band_ref, out_ref, seg_ref, acc_ref, tile_ref):
    step = pl.program_id(0)
    spans, channels, samples = rows_ref.shape
    columns = samples // LANES
    lane = lax.broadcasted_iota(jnp.int32, (channels, LANES), 1)

    def one_segment(s, carry):
        start = starts_ref[s]
        within = lax.rem(start, LANES)
        first = start // LANES + step * (DEPTH // LANES)
        turn = lax.rem(LANES - within, LANES)
        row = pl.ds(pl.multiple_of(s * channels, channels), channels)
        turned = []
        for t in range(DEPTH // LANES + 1):
            column = jnp.minimum(first + t, spans * columns - 1)
            at = pl.ds(pl.multiple_of(lax.rem(column, columns) * LANES, LANES), LANES)
            piece = rows_ref[column // columns, :, at].astype(jnp.float32)
            turned.append(pltpu.roll(piece, turn, 1))
        for t in range(DEPTH // LANES):
            piece = jnp.where(lane < LANES - within, turned[t], turned[t + 1]).astype(jnp.bfloat16)
            seg_ref[row, t * LANES : (t + 1) * LANES] = piece
            seg_ref[row, DEPTH + t * LANES : DEPTH + (t + 1) * LANES] = piece
        return carry

    lax.fori_loop(0, starts_ref.shape[0], one_segment, 0)

    @pl.when(step == 0)
    def _():
        acc_ref[...] = jnp.zeros_like(acc_ref)

    for c in range(0, 2 * WIDE, 256):
        acc_ref[:, c : c + 256] += jnp.dot(
            seg_ref[...], table_ref[0, :, c : c + 256], preferred_element_type=jnp.float32
        )

    @pl.when(step == STEPS - 1)
    def _():
        block = tile_ref.shape[1] // FOLD

        def whiten(b, carry):
            row = pl.ds(pl.multiple_of(b * block, block), block)
            real = acc_ref[row, :WIDE]
            imag = acc_ref[row, WIDE:]
            power = real * real + imag * imag
            high = power.astype(jnp.bfloat16)
            low = (power - high.astype(jnp.float32)).astype(jnp.bfloat16)
            total = jnp.dot(high, band_ref[...], preferred_element_type=jnp.float32)
            total += jnp.dot(low, band_ref[...], preferred_element_type=jnp.float32)
            inverse = lax.rsqrt(total * (1.0 / (2 * HALF + 1)) + 1e-06)
            tiles = pl.ds(pl.multiple_of(b * block * FOLD, block * FOLD), block * FOLD)
            for part, values in enumerate((real, imag)):
                scaled = values[:, :BINS] * inverse
                for s in range(block // channels):
                    first = s // 2 * channels * PAIR + s % 2 * FOLD
                    for g in range(FOLD):
                        tile_ref[part, pl.ds(first + g, channels, stride=PAIR), :] = scaled[
                            s * channels : (s + 1) * channels, g * LANES : (g + 1) * LANES
                        ]
                out_ref[part, tiles, :] = tile_ref[part].astype(jnp.bfloat16)
            return carry

        lax.fori_loop(0, acc_ref.shape[0] // block, whiten, 0)


def whitened(regrouped, seg_starts):
    _, channels, _ = regrouped.shape
    rows = channels * seg_starts.shape[0]
    return pl.pallas_call(
        spectra_kernel,
        grid=(STEPS,),
        in_specs=[
            pl.BlockSpec(memory_space=pltpu.SMEM),
            pl.BlockSpec(regrouped.shape, lambda j: (0, 0, 0)),
            pl.BlockSpec((1, 2 * DEPTH, 2 * WIDE), lambda j: (j, 0, 0)),
            pl.BlockSpec((WIDE, BINS), lambda j: (0, 0)),
        ],
        out_specs=pl.BlockSpec((2, rows * FOLD, LANES), lambda j: (0, 0, 0)),
        out_shape=jax.ShapeDtypeStruct((2, rows * FOLD, LANES), jnp.bfloat16),
        scratch_shapes=[
            pltpu.VMEM((rows, 2 * DEPTH), jnp.bfloat16),
            pltpu.VMEM((rows, 2 * WIDE), jnp.float32),
            pltpu.VMEM((2, 128 * FOLD, LANES), jnp.float32),
        ],
        compiler_params=pltpu.CompilerParams(vmem_limit_bytes=56 * 2**20),
        cost_estimate=pl.CostEstimate(
            flops=2 * rows * 2 * L * 2 * WIDE, transcendentals=0, bytes_accessed=80 * 2**20
        ),
    )(seg_starts, regrouped, jnp.asarray(forward_tables()), jnp.asarray(band_table()))


def pairs_kernel(segs, channels, partners, scale, *refs):
    pieces = len(refs) - 6
    offsets_ref = refs[0]
    piece_refs = refs[1 : 1 + pieces]
    lag_ref, out_ref, ext_ref, real_ref, imag_ref = refs[1 + pieces :]
    total = pieces * channels
    block = out_ref.shape[0] // partners
    step = pl.program_id(0)

    @pl.when(step == 0)
    def _():
        for p, piece_ref in enumerate(piece_refs):

            def fill(ps, carry, p=p, piece_ref=piece_ref):
                length = channels * PAIR
                source = pl.ds(pl.multiple_of(ps * length, length), length)
                base = pl.multiple_of((ps * total + p * channels) * PAIR, length)
                ext_ref[pl.ds(base, length), :] = piece_ref[source, :]
                return carry

            lax.fori_loop(0, segs, fill, 0)

    def tile(part, s, channel):
        at = ((part * (segs // 2) + s) * total + channel) * PAIR
        return ext_ref[pl.ds(pl.multiple_of(at, PAIR), PAIR), :]

    def halves(packed):
        wide = packed.astype(jnp.float32)
        return wide[:FOLD] + wide[FOLD:]

    together = 8

    def some_pairs(n, carry):
        local = n // (partners // together)
        k0 = lax.rem(n, partners // together) * together
        own = step * block + local
        others = [own + offsets_ref[own, k0 + u] for u in range(together)]
        reals = [None] * together
        imags = [None] * together
        for s0 in range(0, segs // 2, 4):
            part_real = [[] for _ in range(together)]
            part_imag = [[] for _ in range(together)]
            for s in range(s0, s0 + 4):
                ar = tile(0, s, own)
                ai = tile(1, s, own)
                for u in range(together):
                    br = tile(0, s, others[u])
                    bi = tile(1, s, others[u])
                    part_real[u].append(ar * br + ai * bi)
                    part_imag[u].append(ai * br - ar * bi)
            for u in range(together):
                a, b, c, d = part_real[u]
                real = halves((a + b) + (c + d))
                a, b, c, d = part_imag[u]
                imag = halves((a + b) + (c + d))
                reals[u] = real if s0 == 0 else reals[u] + real
                imags[u] = imag if s0 == 0 else imags[u] + imag
        for u in range(together):
            at = pl.ds(pl.multiple_of((n * together + u) * FOLD, FOLD), FOLD)
            real_ref[at, :] = reals[u]
            imag_ref[at, :] = imags[u]
        return carry

    lax.fori_loop(0, block * partners // together, some_pairs, 0)

    rows = block * partners
    result = jnp.zeros((rows, LAGS), jnp.float32)
    for g in range(FOLD):
        real = real_ref[pl.ds(g, rows, stride=FOLD), :]
        imag = imag_ref[pl.ds(g, rows, stride=FOLD), :]
        both = jnp.concatenate([real, imag], axis=1).astype(jnp.bfloat16)
        result += jnp.dot(both, lag_ref[g], preferred_element_type=jnp.float32)
    out_ref[...] = (result * scale).astype(jnp.bfloat16)


def correlate(pieces, offsets, segs):
    channels, partners = offsets.shape
    block = 8 if channels % 8 == 0 else channels
    rows = block * partners
    total = len(pieces) * channels
    scale = 1.0 / math.sqrt(segs * BINS)
    return pl.pallas_call(
        functools.partial(pairs_kernel, segs, channels, partners, scale),
        grid=(channels // block,),
        in_specs=[pl.BlockSpec(memory_space=pltpu.SMEM)]
        + [pl.BlockSpec(piece.shape, lambda i: (0, 0)) for piece in pieces]
        + [pl.BlockSpec((FOLD, 2 * LANES, LAGS), lambda i: (0, 0, 0))],
        out_specs=pl.BlockSpec((rows, LAGS), lambda i: (i, 0)),
        out_shape=jax.ShapeDtypeStruct((channels * partners, LAGS), jnp.bfloat16),
        scratch_shapes=[
            pltpu.VMEM((segs * total * PAIR, LANES), jnp.bfloat16),
            pltpu.VMEM((rows * FOLD, LANES), jnp.float32),
            pltpu.VMEM((rows * FOLD, LANES), jnp.float32),
        ],
        compiler_params=pltpu.CompilerParams(vmem_limit_bytes=56 * 2**20),
        cost_estimate=pl.CostEstimate(
            flops=channels * partners * segs * 8 * BINS,
            transcendentals=0,
            bytes_accessed=80 * 2**20,
        ),
    )(offsets, *pieces, jnp.asarray(lag_table()))


def on_device(traces, seg_starts, pair_offsets):
    span = lax.axis_size("span")
    channels_here = traces.shape[0] // span
    segs = seg_starts.shape[0]
    chunk = channels_here // CHUNKS
    halo = MAXOFF // chunk
    by_chunk = traces.reshape(span, CHUNKS, chunk, traces.shape[1])
    pieces = []
    regrouped = []
    for h in range(CHUNKS):
        regrouped.append(
            lax.all_to_all(by_chunk[:, h], "span", split_axis=0, concat_axis=0, tiled=True)
        )
    for h in range(CHUNKS):
        rows = regrouped[h]
        if pieces:
            rows, pieces[-1] = lax.optimization_barrier((rows, pieces[-1]))
        spectra = whitened(rows, seg_starts)
        pieces.append(spectra.reshape(2 * segs * chunk * FOLD, LANES))
    last = CHUNKS + halo
    pieces += [None] * halo
    arrived = []
    for h in range(CHUNKS):
        piece = pieces[h]
        if arrived:
            piece = lax.optimization_barrier((piece, *arrived))[0]
        arrived = []
        for ahead in range(CHUNKS + h, last, CHUNKS):
            pieces[ahead] = passed_along(piece, ("grp", "span"), -(ahead // CHUNKS))
            arrived.append(pieces[ahead])
    results = []
    for h in range(CHUNKS):
        offsets = pair_offsets[h * chunk : (h + 1) * chunk]
        results.append(correlate(pieces[h : h + halo + 1], offsets, segs))
    result = jnp.concatenate(results, axis=0)
    return result.reshape(channels_here, pair_offsets.shape[1], LAGS)


def solution(mesh):
    placed = (P("grp", "span"), P(), P(("grp", "span"), None))
    return jax.shard_map(
        on_device,
        mesh=mesh,
        in_specs=placed,
        out_specs=P(("grp", "span"), None, None),
        check_vma=False,
    )
```

```python
import functools
import math

import jax
import jax.numpy as jnp
import ml_dtypes
import numpy as np
from jax import lax
from jax.experimental import pallas as pl
from jax.experimental.pallas import tpu as pltpu
from jax.sharding import PartitionSpec as P

L = 4096
BINS = 1024
BIN0 = 64
HALF = 32
LAGS = 512
MAXOFF = 64

LANES = 128
WIDE = 1152
DEPTH = 512
STEPS = L // DEPTH
FOLD = BINS // LANES
PAIR = 2 * FOLD
CHUNKS = 2


def passed_along(block, axis, distance):
    devices = range(lax.axis_size(axis))
    route = [(i - distance, i) for i in devices if i - distance in devices]
    return lax.ppermute(block, axis, route)


@functools.cache
def column_bins():
    band = np.arange(BIN0, BIN0 + BINS)
    below = np.arange(BIN0 - HALF, BIN0)
    above = np.arange(BIN0 + BINS, BIN0 + BINS + HALF)
    return np.concatenate([band, below, above])


@functools.cache
def forward_tables():
    bins = column_bins()
    n = np.arange(L)
    angles = (n[:, None] * bins[None, :] % L) * (2.0 * np.pi / L)
    taper = (0.5 - 0.5 * np.cos(2.0 * np.pi / L * (n + 0.5)))[:, None]
    table = np.zeros((L, 2 * WIDE), np.float32)
    table[:, : len(bins)] = np.cos(angles) * taper
    table[:, WIDE : WIDE + len(bins)] = -np.sin(angles) * taper
    high = table.astype(ml_dtypes.bfloat16)
    low = (table - high.astype(np.float32)).astype(ml_dtypes.bfloat16)
    both = np.stack([high.reshape(STEPS, DEPTH, -1), low.reshape(STEPS, DEPTH, -1)], axis=1)
    return both.reshape(STEPS, 2 * DEPTH, 2 * WIDE)


@functools.cache
def band_table():
    bins = column_bins()
    band = np.zeros((WIDE, BINS), np.float32)
    centre = np.arange(BINS) + BIN0
    band[: len(bins)] = np.abs(bins[:, None] - centre[None, :]) <= HALF
    return band.astype(ml_dtypes.bfloat16)


@functools.cache
def lag_table():
    bins = np.arange(BINS) + BIN0
    lags = np.arange(LAGS) - LAGS // 2
    angles = (bins[:, None] * lags[None, :] % L) * (2.0 * np.pi / L)
    table = np.stack([np.cos(angles), -np.sin(angles)]).reshape(2, FOLD, LANES, LAGS)
    table = table.transpose(1, 0, 2, 3).reshape(FOLD, 2 * LANES, LAGS)
    return table.astype(np.float32).astype(ml_dtypes.bfloat16)


def spectra_kernel(starts_ref, rows_ref, table_ref, band_ref, out_ref, seg_ref, acc_ref, tile_ref):
    step = pl.program_id(0)
    spans, channels, samples = rows_ref.shape
    columns = samples // LANES
    lane = lax.broadcasted_iota(jnp.int32, (channels, LANES), 1)

    def one_segment(s, carry):
        start = starts_ref[s]
        within = lax.rem(start, LANES)
        first = start // LANES + step * (DEPTH // LANES)
        turn = lax.rem(LANES - within, LANES)
        row = pl.ds(pl.multiple_of(s * channels, channels), channels)
        turned = []
        for t in range(DEPTH // LANES + 1):
            column = jnp.minimum(first + t, spans * columns - 1)
            at = pl.ds(pl.multiple_of(lax.rem(column, columns) * LANES, LANES), LANES)
            piece = rows_ref[column // columns, :, at].astype(jnp.float32)
            turned.append(pltpu.roll(piece, turn, 1))
        for t in range(DEPTH // LANES):
            piece = jnp.where(lane < LANES - within, turned[t], turned[t + 1]).astype(jnp.bfloat16)
            seg_ref[row, t * LANES : (t + 1) * LANES] = piece
            seg_ref[row, DEPTH + t * LANES : DEPTH + (t + 1) * LANES] = piece
        return carry

    lax.fori_loop(0, starts_ref.shape[0], one_segment, 0)

    @pl.when(step == 0)
    def _():
        acc_ref[...] = jnp.zeros_like(acc_ref)

    for c in range(0, 2 * WIDE, 256):
        acc_ref[:, c : c + 256] += jnp.dot(
            seg_ref[...], table_ref[0, :, c : c + 256], preferred_element_type=jnp.float32
        )

    @pl.when(step == STEPS - 1)
    def _():
        block = tile_ref.shape[1] // FOLD

        def whiten(b, carry):
            row = pl.ds(pl.multiple_of(b * block, block), block)
            real = acc_ref[row, :WIDE]
            imag = acc_ref[row, WIDE:]
            power = real * real + imag * imag
            high = power.astype(jnp.bfloat16)
            low = (power - high.astype(jnp.float32)).astype(jnp.bfloat16)
            total = jnp.dot(high, band_ref[...], preferred_element_type=jnp.float32)
            total += jnp.dot(low, band_ref[...], preferred_element_type=jnp.float32)
            inverse = lax.rsqrt(total * (1.0 / (2 * HALF + 1)) + 1e-06)
            tiles = pl.ds(pl.multiple_of(b * block * FOLD, block * FOLD), block * FOLD)
            for part, values in enumerate((real, imag)):
                scaled = values[:, :BINS] * inverse
                for s in range(block // channels):
                    first = s // 2 * channels * PAIR + s % 2 * FOLD
                    for g in range(FOLD):
                        tile_ref[part, pl.ds(first + g, channels, stride=PAIR), :] = scaled[
                            s * channels : (s + 1) * channels, g * LANES : (g + 1) * LANES
                        ]
                out_ref[part, tiles, :] = tile_ref[part].astype(jnp.bfloat16)
            return carry

        lax.fori_loop(0, acc_ref.shape[0] // block, whiten, 0)


def whitened(regrouped, seg_starts):
    _, channels, _ = regrouped.shape
    rows = channels * seg_starts.shape[0]
    return pl.pallas_call(
        spectra_kernel,
        grid=(STEPS,),
        in_specs=[
            pl.BlockSpec(memory_space=pltpu.SMEM),
            pl.BlockSpec(regrouped.shape, lambda j: (0, 0, 0)),
            pl.BlockSpec((1, 2 * DEPTH, 2 * WIDE), lambda j: (j, 0, 0)),
            pl.BlockSpec((WIDE, BINS), lambda j: (0, 0)),
        ],
        out_specs=pl.BlockSpec((2, rows * FOLD, LANES), lambda j: (0, 0, 0)),
        out_shape=jax.ShapeDtypeStruct((2, rows * FOLD, LANES), jnp.bfloat16),
        scratch_shapes=[
            pltpu.VMEM((rows, 2 * DEPTH), jnp.bfloat16),
            pltpu.VMEM((rows, 2 * WIDE), jnp.float32),
            pltpu.VMEM((2, 128 * FOLD, LANES), jnp.float32),
        ],
        compiler_params=pltpu.CompilerParams(vmem_limit_bytes=56 * 2**20),
        cost_estimate=pl.CostEstimate(
            flops=2 * rows * 2 * L * 2 * WIDE, transcendentals=0, bytes_accessed=80 * 2**20
        ),
    )(seg_starts, regrouped, jnp.asarray(forward_tables()), jnp.asarray(band_table()))


def pairs_kernel(pieces, segs, channels, partners, scale, *refs):
    offsets_ref = refs[0]
    piece_refs = refs[1 : 1 + pieces]
    lag_ref = refs[1 + pieces]
    out_ref, ext_ref, real_ref, imag_ref = refs[-4:]
    total = pieces * channels
    block = out_ref.shape[0] // partners
    step = pl.program_id(0)

    @pl.when(step == 0)
    def _():
        for p, piece_ref in enumerate(piece_refs):

            def fill(ps, carry, p=p, piece_ref=piece_ref):
                length = channels * PAIR
                source = pl.ds(pl.multiple_of(ps * length, length), length)
                base = pl.multiple_of((ps * total + p * channels) * PAIR, length)
                ext_ref[pl.ds(base, length), :] = piece_ref[source, :]
                return carry

            lax.fori_loop(0, segs, fill, 0)

    def tile(part, s, channel):
        at = ((part * (segs // 2) + s) * total + channel) * PAIR
        return ext_ref[pl.ds(pl.multiple_of(at, PAIR), PAIR), :]

    def halves(packed):
        wide = packed.astype(jnp.float32)
        return wide[:FOLD] + wide[FOLD:]

    together = 8

    def some_pairs(n, carry):
        local = n // (partners // together)
        k0 = lax.rem(n, partners // together) * together
        own = step * block + local
        others = [own + offsets_ref[own, k0 + u] for u in range(together)]
        reals = [None] * together
        imags = [None] * together
        for s0 in range(0, segs // 2, 4):
            part_real = [[] for _ in range(together)]
            part_imag = [[] for _ in range(together)]
            for s in range(s0, s0 + 4):
                ar = tile(0, s, own)
                ai = tile(1, s, own)
                for u in range(together):
                    br = tile(0, s, others[u])
                    bi = tile(1, s, others[u])
                    part_real[u].append(ar * br + ai * bi)
                    part_imag[u].append(ai * br - ar * bi)
            for u in range(together):
                a, b, c, d = part_real[u]
                real = halves((a + b) + (c + d))
                a, b, c, d = part_imag[u]
                imag = halves((a + b) + (c + d))
                reals[u] = real if s0 == 0 else reals[u] + real
                imags[u] = imag if s0 == 0 else imags[u] + imag
        for u in range(together):
            at = pl.ds(pl.multiple_of((n * together + u) * FOLD, FOLD), FOLD)
            real_ref[at, :] = reals[u]
            imag_ref[at, :] = imags[u]
        return carry

    lax.fori_loop(0, block * partners // together, some_pairs, 0)

    rows = block * partners
    result = jnp.zeros((rows, LAGS), jnp.float32)
    for g in range(FOLD):
        real = real_ref[pl.ds(g, rows, stride=FOLD), :]
        imag = imag_ref[pl.ds(g, rows, stride=FOLD), :]
        both = jnp.concatenate([real, imag], axis=1).astype(jnp.bfloat16)
        result += jnp.dot(both, lag_ref[g], preferred_element_type=jnp.float32)
    out_ref[...] = (result * scale).astype(jnp.bfloat16)


def correlate(pieces, offsets, segs, part, parts, earlier):
    channels, partners = offsets.shape
    block = 8 if channels % 8 == 0 else channels
    rows = block * partners
    total = len(pieces) * channels
    scale = 1.0 / math.sqrt(segs * BINS)
    first = part * (channels // block)
    return pl.pallas_call(
        functools.partial(pairs_kernel, len(pieces), segs, channels, partners, scale),
        grid=(channels // block,),
        in_specs=[pl.BlockSpec(memory_space=pltpu.SMEM)]
        + [pl.BlockSpec(piece.shape, lambda i: (0, 0)) for piece in pieces]
        + [pl.BlockSpec((FOLD, 2 * LANES, LAGS), lambda i: (0, 0, 0))]
        + [pl.BlockSpec(memory_space=pl.ANY)] * len(earlier),
        out_specs=pl.BlockSpec((rows, LAGS), lambda i: (first + i, 0)),
        out_shape=jax.ShapeDtypeStruct((parts * channels * partners, LAGS), jnp.bfloat16),
        input_output_aliases={len(pieces) + 2: 0} if earlier else {},
        scratch_shapes=[
            pltpu.VMEM((segs * total * PAIR, LANES), jnp.bfloat16),
            pltpu.VMEM((rows * FOLD, LANES), jnp.float32),
            pltpu.VMEM((rows * FOLD, LANES), jnp.float32),
        ],
        compiler_params=pltpu.CompilerParams(vmem_limit_bytes=56 * 2**20),
        cost_estimate=pl.CostEstimate(
            flops=channels * partners * segs * 8 * BINS,
            transcendentals=0,
            bytes_accessed=80 * 2**20,
        ),
    )(offsets, *pieces, jnp.asarray(lag_table()), *earlier)


def on_device(traces, seg_starts, pair_offsets):
    span = lax.axis_size("span")
    channels_here = traces.shape[0] // span
    segs = seg_starts.shape[0]
    chunk = channels_here // CHUNKS
    halo = MAXOFF // chunk
    by_chunk = traces.reshape(span, CHUNKS, chunk, traces.shape[1])
    pieces = []
    regrouped = []
    for h in range(CHUNKS):
        regrouped.append(
            lax.all_to_all(by_chunk[:, h], "span", split_axis=0, concat_axis=0, tiled=True)
        )
    for h in range(CHUNKS):
        rows = regrouped[h]
        if pieces:
            rows, pieces[-1] = lax.optimization_barrier((rows, pieces[-1]))
        spectra = whitened(rows, seg_starts)
        pieces.append(spectra.reshape(2 * segs * chunk * FOLD, LANES))
    last = CHUNKS + halo
    pieces += [None] * halo
    arrived = []
    for h in range(CHUNKS):
        piece = pieces[h]
        if arrived:
            piece = lax.optimization_barrier((piece, *arrived))[0]
        arrived = []
        for ahead in range(CHUNKS + h, last, CHUNKS):
            pieces[ahead] = passed_along(piece, ("grp", "span"), -(ahead // CHUNKS))
            arrived.append(pieces[ahead])
    results = []
    for h in range(CHUNKS):
        offsets = pair_offsets[h * chunk : (h + 1) * chunk]
        wanted = pieces[h : h + halo + 1]
        results = [correlate(wanted, offsets, segs, h, CHUNKS, results)]
    result = results[0]
    return result.reshape(channels_here, pair_offsets.shape[1], LAGS)


def solution(mesh):
    placed = (P("grp", "span"), P(), P(("grp", "span"), None))
    return jax.shard_map(
        on_device,
        mesh=mesh,
        in_specs=placed,
        out_specs=P(("grp", "span"), None, None),
        check_vma=False,
    )
```
